256 devices in a mesh: req: 32 (over x, z_lo, core), tp: 8 (over y, z_hi).
Axes of the slice: x: 4, y: 4, z: 8 (z_hi: 2, z_lo: 4; z = z_hi * 4 + z_lo), core: 2. Of those that a mesh axis runs over, the one named last changes fastest.
Arguments:
- queries: bfloat16 [4096, 4096], P('req', 'tp'), may hold values from -12 to 12
- keys_values: bfloat16 [4096, 1024], P('req', 'tp'), may hold values from -12 to 12
- segments: int32 [4096], P('req'), may hold values from 0 to 2, as said below
- sink_logits: float32 [64], P('tp'), may hold values from 0 to 4
- out_weight: bfloat16 [4096, 2880], P('tp'), may hold values from -0.09375 to 0.09375
- out_bias: bfloat16 [2880], replicated, may hold values from -3 to 3
- residual: bfloat16 [4096, 2880], P(('req', 'tp')), may hold values from -6 to 6
- norm_gain: bfloat16 [2880], replicated, may hold values from 0.5 to 1.5
- route_ids: int32 [4096, 4], P(('req', 'tp')), may hold values from 0 to 31, all different within a row; in each aligned block of 16 rows (0 to 15, 16 to 31, ...) at most 4 rows name the same one
- route_logits: float32 [4096, 4], P(('req', 'tp')), may hold values from -6 to 6
- gate_weight: bfloat16 [32, 2880, 2880], P('req', None, 'tp'), may hold values from -0.3125 to 0.3125
- gate_bias: bfloat16 [32, 2880], P('req', 'tp'), may hold values from -3 to 3
- up_weight: bfloat16 [32, 2880, 2880], P('req', None, 'tp'), may hold values from -0.3125 to 0.3125
- up_bias: bfloat16 [32, 2880], P('req', 'tp'), may hold values from -3 to 3
- down_weight: bfloat16 [32, 2880, 2880], P('req', 'tp'), may hold values from -0.0546875 to 0.0546875
- down_bias: bfloat16 [32, 2880], replicated, may hold values from -3 to 3
- page_table: int32 [32, 8], P('req'), may hold values from 0 to 7, each once within a row
Outputs:
- mixed_out: bfloat16 [4096, 2880], P(('req', 'tp'))
- kv_cache: bfloat16 [256, 16, 1024], P('req', None, 'tp')
The draws below stay inside these ranges and needn't reach their ends.
Inputs may be any that keep to these rules, and one draw needn't show every extreme that they name: `segments`: within each group of 128 tokens the numbers start at 0, never fall and rise by at most one from token to token; every group holds exactly 3 packed requests, of uneven lengths. `route_ids`: each row names 4 different experts. Among the 16 rows of one device no expert is named by more than 4 rows, a bound that some block reaches. `page_table`: each row names every page of its group once.
All inputs are finite; a program needn't handle non-finite values.
Results may differ from the reference program's by a relative error of at most 0.018.
Values may be sent and summed in bfloat16 or wider, within the bound.
A program may use at most 64 MiB of HBM per device.

```python
import math
import jax
import jax.numpy as jnp
import numpy as np
from jax import lax

D = 2880
FF = 2880
Q_HEADS = 64
KV_HEADS = 8
HEAD = 64
TOP = 4
PAGE_LEN = 16
TOK_DEV = 16
TOK_REQ = 128
TOKENS = 4096
EXPERTS = 32
CAP = 4
PAGES = 8
N_REQ = 32
N_TP = 8


def seg_table(key):
    groups = TOKENS // TOK_REQ
    cuts = 2
    slots = jnp.broadcast_to(jnp.arange(TOK_REQ, dtype=jnp.int32)[None, :], (groups, TOK_REQ))
    shuffled = jax.random.permutation(jax.random.fold_in(key, 11), slots, axis=1, independent=True)
    later_cols = jnp.arange(TOK_REQ, dtype=jnp.int32)[None, :] > 0
    boundary = (shuffled < cuts) & later_cols
    extra = (shuffled == cuts) & later_cols
    zero_cut = jnp.any(shuffled[:, :1] < cuts, axis=1, keepdims=True)
    boundary = boundary | extra & zero_cut
    return jnp.cumsum(boundary.astype(jnp.int32), axis=1).astype(jnp.int32).reshape(TOKENS)


def draw_segments(key, part):
    return seg_table(key)


def attention_inputs(key):
    query_width = Q_HEADS * HEAD
    pair_width = KV_HEADS * 2 * HEAD
    queries = jnp.clip(jax.random.normal(jax.random.fold_in(key, 21), (TOKENS, query_width)), -6.0, 6.0)
    keyvals = jnp.clip(jax.random.normal(jax.random.fold_in(key, 22), (TOKENS, pair_width)), -6.0, 6.0)
    return (queries, keyvals)


def draw_queries(key, part):
    return attention_inputs(key)[0].astype(jnp.bfloat16)


def draw_keys_values(key, part):
    return attention_inputs(key)[1].astype(jnp.bfloat16)


def levels(key, extent, cuts, least, largest):
    def one(dim, blocks):
        heights = jax.random.uniform(jax.random.fold_in(jax.random.fold_in(key, 6), dim), (blocks,), jnp.float32, least / len(cuts), largest / len(cuts))
        return jnp.repeat(jnp.exp(heights), extent[dim] // blocks).reshape((-1,) + (1,) * (len(extent) - dim - 1))

    loudness = one(*cuts[0])
    for cut in cuts[1:]:
        loudness = loudness * one(*cut)
    return loudness


def deal_out(stream_key, own, number, rows, number_of, top, reach, skew):
    order = jax.random.permutation(stream_key, number_of)
    heavy_load, ordinary = shares(number_of, rows * top, reach, skew, True), shares(number_of, rows * top, reach, skew, False)
    places = jnp.arange(number_of)

    def named(sizes, rotation):
        used = int((sizes > 0).sum())
        fixed = max(1, used // 4)
        moved = fixed + (places - fixed + rotation * (used - fixed)) % max(1, number_of - fixed)
        return jnp.zeros((number_of,), jnp.int32).at[order[jnp.where(places < fixed, places, moved)]].set(jnp.asarray(sizes, jnp.int32))

    sizes = jnp.where(number % 4 == 0, named(heavy_load, number // 4), named(ordinary, number - number // 4 - 1))
    mixed = jax.random.permutation(jax.random.fold_in(own, 3), number_of)
    giver, receiver = mixed[0:number_of // 2 * 2:2], mixed[1:number_of // 2 * 2:2]
    margin = jnp.minimum(sizes[giver] - 1, reach - sizes[receiver]) // 2
    margin = jnp.where((giver == order[0]) | (receiver == order[0]) | (sizes[receiver] == 0), 0, jnp.maximum(margin, 0))
    moved = jax.random.randint(jax.random.fold_in(own, 4), (number_of // 2,), 0, 1 << 20) % (margin + 1)
    sizes = sizes.at[giver].add(-moved).at[receiver].add(moved)
    labels = jnp.searchsorted(jnp.cumsum(sizes), jnp.arange(rows * top), side="right").astype(jnp.int32)
    grid = labels.reshape(top, rows).T
    grid = grid[jax.random.permutation(jax.random.fold_in(own, 1), rows)]
    rotation = jax.random.randint(jax.random.fold_in(own, 2), (rows, 1), 0, top)
    return jnp.take_along_axis(grid, (jnp.arange(top)[None, :] + rotation) % top, axis=1)


def shares(amount, total, bound, slope, full):
    weights = [(1 << 20) // math.isqrt(grade ** slope) + 1 for grade in range(1, amount + 1)]
    largest = bound if full else min(bound, max(-(-total // amount), total * weights[0] // sum(weights)))
    least = 1 if total - largest >= amount - 1 else 0
    counts, rest = [largest] + [least] * (amount - 1), total - largest - least * (amount - 1)
    while rest > 0:
        candidates = [i for i in range(1, amount) if counts[i] < largest] or [i for i in range(1, amount) if counts[i] < bound]
        mass, remaining = sum([weights[i] for i in candidates]), rest
        for i in candidates:
            addition = min(bound - counts[i], max(1, remaining * weights[i] // mass), rest)
            counts[i] = counts[i] + addition
            rest = rest - addition
    return np.array(counts)


def normal_values(key, shape, deviation, limit, cuts=(), held_as=jnp.bfloat16):
    values = jax.random.normal(key, shape, jnp.float32) * deviation
    if len(cuts) > 0:
        values = levels(key, shape, cuts, -0.22, 0.18) * values
    return jnp.clip(values, min=-limit, max=limit).astype(held_as)


def setup_inputs(seed: int = 0) -> dict:
    seeds = jax.random.split(jax.random.key(seed), 18)
    queries = draw_queries(jax.random.fold_in(seeds[17], 71), 0)
    keys_values = draw_keys_values(jax.random.fold_in(seeds[17], 71), 0)
    segments = draw_segments(jax.random.fold_in(seeds[17], 71), 0)
    sink_logits = jnp.clip(4.0 * jax.random.uniform(seeds[3], (Q_HEADS,), jnp.float32) ** levels(seeds[3], (Q_HEADS,), ((0, 8),), -0.2, 0.2), 0.0, 4.0)
    out_weight = normal_values(seeds[4], (Q_HEADS * HEAD, D), (Q_HEADS * HEAD) ** -0.5, 0.09375, ((0, 8),))
    out_bias = normal_values(seeds[5], (D,), 0.5, 3.0)
    residual = normal_values(seeds[6], (TOKENS, D), 1.0, 6.0, ((0, 256),))
    norm_gain = jnp.clip(1.0 + 0.1 * jax.random.normal(seeds[7], (D,), jnp.float32), 0.5, 1.5).astype(jnp.bfloat16)
    route_ids_keys = jax.random.split(jax.random.fold_in(seeds[8], 1), TOKENS // TOK_DEV)
    route_ids_turns = jax.random.permutation(jax.random.fold_in(seeds[8], 3), TOKENS // TOK_DEV)
    route_ids = jax.vmap(lambda own, number: deal_out(jax.random.fold_in(seeds[8], 2), own, number, TOK_DEV, EXPERTS, TOP, CAP, 2))(route_ids_keys, route_ids_turns).reshape((TOKENS, TOP))
    route_logits = normal_values(seeds[9], (TOKENS, TOP), 1.5, 6.0, ((0, 256),), jnp.float32)
    gate_weight = normal_values(seeds[10], (EXPERTS, D, FF), (D // 8) ** -0.5, 0.3125, ((0, 32), (2, 8)))
    gate_bias = normal_values(seeds[11], (EXPERTS, FF), 0.5, 3.0, ((0, 32), (1, 8)))
    up_weight = normal_values(seeds[12], (EXPERTS, D, FF), (D // 8) ** -0.5, 0.3125, ((0, 32), (2, 8)))
    up_bias = normal_values(seeds[13], (EXPERTS, FF), 0.5, 3.0, ((0, 32), (1, 8)))
    down_weight = normal_values(seeds[14], (EXPERTS, FF, D), (4 * FF) ** -0.5, 0.0546875, ((0, 32), (1, 8)))
    down_bias = normal_values(seeds[15], (EXPERTS, D), 0.5, 3.0)
    page_table = jax.vmap(lambda own: jax.random.permutation(own, PAGES))(jax.random.split(seeds[16], N_REQ)).reshape((N_REQ, PAGES)).astype(jnp.int32)
    return {"queries": queries, "keys_values": keys_values, "segments": segments, "sink_logits": sink_logits, "out_weight": out_weight, "out_bias": out_bias, "residual": residual, "norm_gain": norm_gain, "route_ids": route_ids, "route_logits": route_logits, "gate_weight": gate_weight, "gate_bias": gate_bias, "up_weight": up_weight, "up_bias": up_bias, "down_weight": down_weight, "down_bias": down_bias, "page_table": page_table}


rope_base = 150000.0
norm_eps = 1e-05
swiglu_limit = 7.0
glu_alpha = 1.702

def seg_positions(segment_ids):
    length = segment_ids.shape[0]
    indices = jnp.arange(length, dtype=jnp.int32)
    change = jnp.concatenate([jnp.ones((1,), dtype=bool), segment_ids[1:] != segment_ids[:-1]])
    starts = lax.cummax(jnp.where(change, indices, 0).astype(jnp.int32), axis=0)
    return indices - starts

def rotate(values, positions):
    half_dim = values.shape[-1] // 2
    inverse = rope_base ** (-jnp.arange(half_dim, dtype=jnp.float32) / half_dim)
    angles = positions.astype(jnp.float32)[:, None] * inverse[None, :]
    cosine = jnp.cos(angles)[:, None, :]
    sine_col = jnp.sin(angles)[:, None, :]
    first_half = values[..., :half_dim]
    second_half = values[..., half_dim:]
    return jnp.concatenate([first_half * cosine - second_half * sine_col, second_half * cosine + first_half * sine_col], axis=-1)

def attend_group(queries, keys_values, segment_ids, sink_logits):
    length = queries.shape[0]
    kv_heads = keys_values.shape[1] // (2 * HEAD)
    q_heads = queries.shape[1] // HEAD
    group_size = q_heads // kv_heads
    positions = seg_positions(segment_ids)
    q_rot = rotate(queries.astype(jnp.float32).reshape(length, q_heads, HEAD), positions).astype(jnp.bfloat16)
    q_rot = q_rot.reshape(length, kv_heads, group_size, HEAD)
    key_part = keys_values.reshape(length, kv_heads, 2, HEAD)
    k_rot = rotate(key_part[:, :, 0].astype(jnp.float32), positions).astype(jnp.bfloat16)
    values = key_part[:, :, 1]
    scores = jnp.einsum('qkgd,skd->kgqs', q_rot.astype(jnp.float32), k_rot.astype(jnp.float32)) * HEAD ** (-0.5)
    indices = jnp.arange(length, dtype=jnp.int32)
    visible = (segment_ids[:, None] == segment_ids[None, :]) & (indices[None, :] <= indices[:, None])
    scores = jnp.where(visible, scores, -jnp.inf)
    sink_col = sink_logits.reshape(kv_heads, group_size)[:, :, None]
    highest = jnp.maximum(lax.optimization_barrier(jnp.max(scores, axis=-1)), sink_col)
    expo_terms = jnp.exp(scores - highest[..., None])
    denominator = lax.optimization_barrier(jnp.sum(expo_terms, axis=-1)) + jnp.exp(sink_col - highest)
    probabilities = (expo_terms / denominator[..., None]).astype(jnp.bfloat16)
    attended = jnp.einsum('kgqs,skd->qkgd', probabilities.astype(jnp.float32), values.astype(jnp.float32))
    attended = attended.astype(jnp.bfloat16).reshape(length, q_heads * HEAD)
    cached = jnp.stack([k_rot, values], axis=2).reshape(length, kv_heads * 2 * HEAD)
    return (attended, cached)

def reference(queries, keys_values, segments, sink_logits, out_weight, out_bias, residual, norm_gain, route_ids, route_logits, gate_weight, gate_bias, up_weight, up_bias, down_weight, down_bias, page_table):

    def one_group(pieces):
        return attend_group(pieces[0], pieces[1], pieces[2], sink_logits)
    attended, cached = lax.map(one_group, (queries.reshape(N_REQ, TOK_REQ, -1), keys_values.reshape(N_REQ, TOK_REQ, -1), segments.reshape(N_REQ, TOK_REQ)))
    attended = attended.reshape(TOKENS, -1)
    projected = jnp.dot(attended, out_weight, preferred_element_type=jnp.float32)
    hidden = (residual.astype(jnp.float32) + projected + out_bias.astype(jnp.float32)).astype(jnp.bfloat16)
    stream = hidden.astype(jnp.float32)
    normed = (stream * lax.rsqrt(lax.optimization_barrier(jnp.mean(stream * stream, axis=-1, keepdims=True)) + norm_eps) * norm_gain.astype(jnp.float32)).astype(jnp.bfloat16)
    route_weights = jax.nn.softmax(route_logits.astype(jnp.float32), axis=-1)
    capacity = N_REQ * N_TP * CAP

    def expert_step(carry, pieces):
        w_gate, b_gate, w_up, b_up, w_down, b_down, expert = pieces
        hit = route_ids == expert
        chosen = jnp.any(hit, axis=1)
        share = lax.optimization_barrier(jnp.sum(jnp.where(hit, route_weights, 0.0), axis=1))
        order = jnp.cumsum(chosen.astype(jnp.int32)) - 1
        chosen_count = jnp.sum(chosen.astype(jnp.int32))
        target = jnp.where(chosen, order, capacity).astype(jnp.int32)
        member = jnp.zeros((capacity,), jnp.int32).at[target].set(jnp.arange(TOKENS, dtype=jnp.int32), mode='drop')
        valid = jnp.arange(capacity, dtype=jnp.int32) < chosen_count
        picked = normed[member]
        gate_act = jnp.dot(picked, w_gate, preferred_element_type=jnp.float32) + b_gate.astype(jnp.float32)
        up_act = jnp.dot(picked, w_up, preferred_element_type=jnp.float32) + b_up.astype(jnp.float32)
        gate_act = jnp.minimum(gate_act, swiglu_limit)
        up_act = jnp.clip(up_act, -swiglu_limit, swiglu_limit)
        active = (gate_act * jax.nn.sigmoid(glu_alpha * gate_act) * (up_act + 1.0)).astype(jnp.bfloat16)
        partial_value = jnp.einsum('rtf,tfd->trd', active.reshape(capacity, N_TP, -1).astype(jnp.float32), w_down.reshape(N_TP, -1, D).astype(jnp.float32))
        rounded = lax.optimization_barrier(partial_value.astype(jnp.bfloat16))
        expert_out = lax.optimization_barrier(jnp.sum(rounded.astype(jnp.float32), axis=0)) + b_down.astype(jnp.float32)
        scale = jnp.where(valid, share[member], 0.0)
        return (carry.at[member].add(scale[:, None] * expert_out), None)
    expert_mix, _ = lax.scan(expert_step, jnp.zeros((TOKENS, D), jnp.float32), (gate_weight, gate_bias, up_weight, up_bias, down_weight, down_bias, jnp.arange(EXPERTS, dtype=jnp.int32)))
    mixed_out = (stream + expert_mix).astype(jnp.bfloat16)
    blocks = cached.reshape(N_REQ, PAGES, PAGE_LEN, -1)

    def place_pages(table, block_set):
        return jnp.zeros_like(block_set).at[table].set(block_set)
    page_pool = jax.vmap(place_pages)(page_table, blocks).reshape(N_REQ * PAGES, PAGE_LEN, -1)
    return (mixed_out, page_pool)
```

```python
import functools

import jax
import jax.numpy as jnp
from jax import lax
from jax.experimental import pallas as pl
from jax.experimental.pallas import tpu as pltpu
from jax.sharding import PartitionSpec as P

HEAD = 64
PAGE_LEN = 16
MESH = pl.DeviceIdType.MESH

rope_base = 150000.0
norm_eps = 1e-05
swiglu_limit = 7.0
glu_alpha = 1.702

X, Y, Z, C = 4, 4, 8, 2
META = 64
F32, BF16 = jnp.float32, jnp.bfloat16


def coords():
    r, t = lax.axis_index("req"), lax.axis_index("tp")
    return r // 8, t // 2, (t % 2) * 4 + (r // 2) % 4, r % 2


def device(x, y, z, c):
    return (x * 8 + (z % 4) * 2 + c, y * 2 + z // 4)


def entry_barrier(peers):
    barrier = pltpu.get_barrier_semaphore()
    for peer in peers:
        pl.semaphore_signal(barrier, inc=1, device_id=peer, device_id_type=MESH)
    pl.semaphore_wait(barrier, len(peers))


def remote(src, dst, send, recv, peer):
    return pltpu.make_async_remote_copy(
        src_ref=src, dst_ref=dst, send_sem=send, recv_sem=recv, device_id=peer, device_id_type=MESH
    )


def vmem(count):
    return [pl.BlockSpec(memory_space=pltpu.VMEM)] * count


def project_kernel(
    part, residual, bias, gain, meta, toks, hidden, from_y, from_z, stage,
    y_send, y_recv, p_send, p_recv, z_send, z_recv, c_send, c_recv,
):
    x, y, z, c = coords()
    zh = z // 4
    width = part.shape[1]
    y_peer = [device(x, (y + d) % Y, z, c) for d in range(Y)]
    z_peer = [device(x, y, (z + d) % Z, c) for d in range(Z)]
    partner = device(x, y, z, 1 - c)
    entry_barrier(y_peer[1:] + z_peer[1:] + [partner])
    sends = []
    for d in (2, 1, 3):
        rows = pl.ds(pl.multiple_of(((y + d) % Y) * 32, 32), 32)
        copy = remote(part.at[rows], from_y.at[d - 1], y_send.at[d - 1], y_recv.at[d - 1], y_peer[d])
        copy.start()
        sends.append(copy)
    for copy in sends:
        copy.wait_recv()

    def summed(half):
        at = pl.multiple_of(half * 16, 16)
        total = part[pl.ds(pl.multiple_of(y * 32 + half * 16, 16), 16), :].astype(F32)
        for d in range(Y - 1):
            total = total + from_y[d, pl.ds(at, 16), :].astype(F32)
        return total

    stage[...] = summed(1 - zh).astype(BF16)
    swap = remote(stage, from_z, p_send, p_recv, z_peer[4])
    swap.start()
    own = summed(zh) + residual[...].astype(F32) + bias[...].astype(F32)
    swap.wait_recv()
    rounded = (own + from_z[...].astype(F32)).astype(BF16)
    hidden[...] = rounded
    stream = rounded.astype(F32)
    scale = lax.rsqrt(jnp.mean(stream * stream, axis=-1, keepdims=True) + norm_eps)
    slot = c * Z + z
    toks[slot, :, 0:width] = (stream * scale * gain[...].astype(F32)).astype(BF16)
    toks[slot, :, width : width + META] = meta[...]
    z_copies = {}
    for d in (4, 3, 5, 2, 6, 1, 7):
        copy = remote(toks.at[slot], toks.at[slot], z_send.at[d - 1], z_recv.at[d - 1], z_peer[d])
        copy.start()
        z_copies[d] = copy
    crossings = []
    for d in (0, 1, 7, 2, 6, 3, 5, 4):
        if d:
            z_copies[d].wait_recv()
        block = c * Z + (z - d + Z) % Z
        copy = remote(toks.at[block], toks.at[block], c_send.at[d], c_recv.at[d], partner)
        copy.start()
        crossings.append(copy)
    for copy in crossings:
        copy.wait_recv()
    for copy in sends + [swap] + list(z_copies.values()) + crossings:
        copy.wait_send()


def project(part, residual, bias, gain, meta):
    width = part.shape[1]
    rows = residual.shape[0]
    return pl.pallas_call(
        project_kernel,
        out_shape=(
            jax.ShapeDtypeStruct((C * Z, rows, width + META), BF16),
            jax.ShapeDtypeStruct((rows, width), BF16),
        ),
        in_specs=vmem(5),
        out_specs=tuple(vmem(2)),
        scratch_shapes=[
            pltpu.VMEM((Y - 1, 2 * rows, width), BF16),
            pltpu.VMEM((rows, width), BF16),
            pltpu.VMEM((rows, width), BF16),
            pltpu.SemaphoreType.DMA((Y - 1,)),
            pltpu.SemaphoreType.DMA((Y - 1,)),
            pltpu.SemaphoreType.DMA,
            pltpu.SemaphoreType.DMA,
            pltpu.SemaphoreType.DMA((Z - 1,)),
            pltpu.SemaphoreType.DMA((Z - 1,)),
            pltpu.SemaphoreType.DMA((Z,)),
            pltpu.SemaphoreType.DMA((Z,)),
        ],
        compiler_params=pltpu.CompilerParams(collective_id=0, has_side_effects=True),
        name="project_gather",
    )(part, residual, bias, gain, meta)


def spread_kernel(chosen, out, x_send, x_recv, local, n_send, n_recv, f_send, f_recv):
    x, y, z, c = coords()
    x_peer = [device((x + d) % X, y, z, c) for d in range(X)]
    right, left = device(x, (y + 1) % Y, z, c), device(x, (y + Y - 1) % Y, z, c)
    entry_barrier(x_peer[1:] + [right, left])
    here = pltpu.make_async_copy(chosen.at[x], out.at[y, x], local)
    here.start()
    x_copies = {}
    for d in (2, 1, 3):
        copy = remote(
            chosen.at[(x + d) % X], out.at[y, x], x_send.at[d - 1], x_recv.at[d - 1], x_peer[d]
        )
        copy.start()
        x_copies[d] = copy
    order = (0, 1, 3, 2)
    copies = {}
    for d in order:
        if d:
            x_copies[d].wait_recv()
        else:
            here.wait()
        block = out.at[y, (x - d + X) % X]
        for way, peer in ((0, right), (1, left)):
            copies[way, d] = remote(block, block, n_send.at[way, d], n_recv.at[way, d], peer)
            copies[way, d].start()
    relays = []
    for d in order:
        for way, peer, origin in ((0, right, (y + Y - 1) % Y), (1, left, (y + 1) % Y)):
            copies[way, d].wait_recv()
            if d % 2 == way:
                block = out.at[origin, (x - d + X) % X]
                copy = remote(block, block, f_send.at[way, d // 2], f_recv.at[way, d // 2], peer)
                copy.start()
                relays.append(copy)
    for copy in relays:
        copy.wait_recv()
    for copy in list(x_copies.values()) + list(copies.values()) + relays:
        copy.wait_send()


def spread(chosen):
    _, rows, width = chosen.shape
    return pl.pallas_call(
        spread_kernel,
        out_shape=jax.ShapeDtypeStruct((Y, X, rows, width), BF16),
        in_specs=vmem(1),
        out_specs=vmem(1)[0],
        scratch_shapes=[
            pltpu.SemaphoreType.DMA((X - 1,)),
            pltpu.SemaphoreType.DMA((X - 1,)),
            pltpu.SemaphoreType.DMA,
            pltpu.SemaphoreType.DMA((2, X)),
            pltpu.SemaphoreType.DMA((2, X)),
            pltpu.SemaphoreType.DMA((2, 2)),
            pltpu.SemaphoreType.DMA((2, 2)),
        ],
        compiler_params=pltpu.CompilerParams(collective_id=1, has_side_effects=True),
        name="slots_spread",
    )(chosen)


def add_rows(target, terms):
    rows = target.shape[0]

    def step(i, carry):
        at = pl.ds(pl.multiple_of(i * 16, 16), 16)
        total = terms[0][at, :].astype(F32)
        for term in terms[1:]:
            total = total + term[at, :].astype(F32)
        target[at, :] = total.astype(BF16)
        return carry

    lax.fori_loop(0, rows // 16, step, 0)


def collect_kernel(
    part, out, passing, sums, final, stage,
    h_send, h_recv, d_send, d_recv, s_send, s_recv, x_send, x_recv,
):
    x, y, z, c = coords()
    x_peer = [device((x + d) % X, y, z, c) for d in range(X)]
    y_right, y_left, y_far = (y + 1) % Y, (y + Y - 1) % Y, (y + 2) % Y
    right, left = device(x, y_right, z, c), device(x, y_left, z, c)
    entry_barrier(x_peer[1:] + [right, left])
    halves, directs, added = {}, {}, {}
    for i in range(2):
        for way, peer in ((0, right), (1, left)):
            halves[way, i] = remote(
                part.at[y_far, 2 * i + way], passing.at[way, i],
                h_send.at[way, i], h_recv.at[way, i], peer,
            )
            halves[way, i].start()
    for i in range(2):
        for way, peer, goal in ((0, right, y_right), (1, left, y_left)):
            block = 2 * i + 1 - way
            directs[way, i] = remote(
                part.at[goal, block], final.at[way, block],
                d_send.at[way, i], d_recv.at[way, i], peer,
            )
            directs[way, i].start()
    for i in range(2):
        for way, peer, goal in ((0, right, y_right), (1, left, y_left)):
            block = 2 * i + way
            halves[way, i].wait_recv()
            add_rows(sums.at[way, i], [part.at[goal, block], passing.at[way, i]])
            added[way, i] = remote(
                sums.at[way, i], final.at[way, block], s_send.at[way, i], s_recv.at[way, i], peer
            )
            added[way, i].start()
    for i in range(2):
        for way in range(2):
            directs[way, i].wait_recv()
    for i in range(2):
        for way in range(2):
            added[way, i].wait_recv()
    x_copies = []
    for d in (2, 1, 3, 0):
        goal = (x + d) % X
        terms = [part.at[y, goal], final.at[0, goal], final.at[1, goal]]
        if d:
            add_rows(stage.at[d - 1], terms)
            copy = remote(
                stage.at[d - 1], out.at[x], x_send.at[d - 1], x_recv.at[d - 1], x_peer[d]
            )
            copy.start()
            x_copies.append(copy)
        else:
            add_rows(out.at[x], terms)
    for copy in x_copies:
        copy.wait_recv()
    for copy in [*halves.values(), *directs.values(), *added.values(), *x_copies]:
        copy.wait_send()


def collect(part):
    _, _, rows, width = part.shape
    pair = [pltpu.SemaphoreType.DMA((2, 2))] * 6
    return pl.pallas_call(
        collect_kernel,
        out_shape=jax.ShapeDtypeStruct((X, rows, width), BF16),
        in_specs=vmem(1),
        out_specs=vmem(1)[0],
        scratch_shapes=[
            pltpu.VMEM((2, 2, rows, width), BF16),
            pltpu.VMEM((2, 2, rows, width), BF16),
            pltpu.VMEM((2, X, rows, width), BF16),
            pltpu.VMEM((X - 1, rows, width), BF16),
            *pair,
            pltpu.SemaphoreType.DMA((X - 1,)),
            pltpu.SemaphoreType.DMA((X - 1,)),
        ],
        compiler_params=pltpu.CompilerParams(collective_id=2, has_side_effects=True),
        name="slots_collect",
    )(part)


def finish_kernel(part, base, mixed, from_core, stage, from_z, c_send, c_recv, z_send, z_recv):
    x, y, z, c = coords()
    z_peer = [device(x, y, (z + d) % Z, c) for d in range(Z)]
    partner = device(x, y, z, 1 - c)
    entry_barrier(z_peer[1:] + [partner])
    order = (4, 3, 5, 2, 6, 1, 7, 0)
    crossings = {}
    for d in order:
        goal = (z + d) % Z
        crossings[d] = remote(
            part.at[(1 - c) * Z + goal], from_core.at[d], c_send.at[d], c_recv.at[d], partner
        )
        crossings[d].start()
    z_copies = []
    for d in order[:-1]:
        crossings[d].wait_recv()
        goal = c * Z + (z + d) % Z
        stage[d - 1] = (part[goal].astype(F32) + from_core[d].astype(F32)).astype(BF16)
        copy = remote(stage.at[d - 1], from_z.at[d - 1], z_send.at[d - 1], z_recv.at[d - 1], z_peer[d])
        copy.start()
        z_copies.append(copy)
    crossings[0].wait_recv()
    total = base[...] + part[c * Z + z].astype(F32) + from_core[0].astype(F32)
    for copy in z_copies:
        copy.wait_recv()
    for d in range(Z - 1):
        total = total + from_z[d].astype(F32)
    mixed[...] = total.astype(BF16)
    for copy in list(crossings.values()) + z_copies:
        copy.wait_send()


def finish(part, base):
    _, rows, width = part.shape
    return pl.pallas_call(
        finish_kernel,
        out_shape=jax.ShapeDtypeStruct((rows, width), BF16),
        in_specs=vmem(2),
        out_specs=vmem(1)[0],
        scratch_shapes=[
            pltpu.VMEM((Z, rows, width), BF16),
            pltpu.VMEM((Z - 1, rows, width), BF16),
            pltpu.VMEM((Z - 1, rows, width), BF16),
            pltpu.SemaphoreType.DMA((Z,)),
            pltpu.SemaphoreType.DMA((Z,)),
            pltpu.SemaphoreType.DMA((Z - 1,)),
            pltpu.SemaphoreType.DMA((Z - 1,)),
        ],
        compiler_params=pltpu.CompilerParams(collective_id=3, has_side_effects=True),
        name="tokens_finish",
    )(part, base)


def seg_positions(segment_ids):
    length = segment_ids.shape[0]
    indices = jnp.arange(length, dtype=jnp.int32)
    change = jnp.concatenate([jnp.ones((1,), dtype=bool), segment_ids[1:] != segment_ids[:-1]])
    starts = lax.cummax(jnp.where(change, indices, 0), axis=0)
    return indices - starts


def rotate(values, positions):
    half_dim = values.shape[-1] // 2
    inverse = rope_base ** (-jnp.arange(half_dim, dtype=jnp.float32) / half_dim)
    angles = positions.astype(jnp.float32)[:, None] * inverse[None, :]
    cosine = jnp.cos(angles)[:, None, :]
    sine_col = jnp.sin(angles)[:, None, :]
    first_half = values[..., :half_dim]
    second_half = values[..., half_dim:]
    return jnp.concatenate(
        [
            first_half * cosine - second_half * sine_col,
            second_half * cosine + first_half * sine_col,
        ],
        axis=-1,
    )


def attend_group(queries, keys_values, segment_ids, sink_logits):
    length = queries.shape[0]
    kv_heads = keys_values.shape[1] // (2 * HEAD)
    q_heads = queries.shape[1] // HEAD
    group_size = q_heads // kv_heads
    positions = seg_positions(segment_ids)
    q_rot = rotate(queries.astype(jnp.float32).reshape(length, q_heads, HEAD), positions).astype(
        jnp.bfloat16
    )
    q_rot = q_rot.reshape(length, kv_heads, group_size, HEAD)
    key_part = keys_values.reshape(length, kv_heads, 2, HEAD)
    k_rot = rotate(key_part[:, :, 0].astype(jnp.float32), positions).astype(jnp.bfloat16)
    values = key_part[:, :, 1]
    scores = jnp.einsum(
        "qkgd,skd->kgqs", q_rot, k_rot, preferred_element_type=jnp.float32
    ) * HEAD ** (-0.5)
    indices = jnp.arange(length, dtype=jnp.int32)
    visible = (segment_ids[:, None] == segment_ids[None, :]) & (
        indices[None, :] <= indices[:, None]
    )
    scores = jnp.where(visible, scores, -jnp.inf)
    sink_col = sink_logits.reshape(kv_heads, group_size)[:, :, None]
    highest = jnp.maximum(jnp.max(scores, axis=-1), sink_col)
    expo_terms = jnp.exp(scores - highest[..., None])
    denominator = jnp.sum(expo_terms, axis=-1) + jnp.exp(sink_col - highest)
    probabilities = (expo_terms / denominator[..., None]).astype(jnp.bfloat16)
    attended = jnp.einsum(
        "kgqs,skd->qkgd", probabilities, values, preferred_element_type=jnp.float32
    )
    attended = attended.astype(jnp.bfloat16).reshape(length, q_heads * HEAD)
    cached = jnp.stack([k_rot, values], axis=2).reshape(length, kv_heads * 2 * HEAD)
    return (attended, cached)


def route_meta(route_ids, route_weights):
    rows, width = route_ids.shape
    flat = route_ids.reshape(-1)
    index = jnp.arange(rows * width)
    same = (flat[:, None] == flat[None, :]) & (index[None, :] < index[:, None])
    place = jnp.sum(same.astype(F32), axis=1).reshape(rows, width)
    high = route_weights.astype(BF16)
    low = (route_weights - high.astype(F32)).astype(BF16)
    blank = jnp.zeros((rows, META - 4 * width), BF16)
    return jnp.concatenate(
        [route_ids.astype(BF16), place.astype(BF16), high, low, blank], axis=1
    )


def body(
    queries,
    keys_values,
    segments,
    sink_logits,
    out_weight,
    out_bias,
    residual,
    norm_gain,
    route_ids,
    route_logits,
    gate_weight,
    gate_bias,
    up_weight,
    up_bias,
    down_weight,
    down_bias,
    page_table,
):
    width = residual.shape[1]
    tok_count, top = route_ids.shape
    experts = down_bias.shape[0]
    capacity = max(2, 2 * tok_count * top // experts)
    attended, cached = attend_group(queries, keys_values, segments, sink_logits)
    part = jnp.dot(attended, out_weight, preferred_element_type=F32).astype(BF16)
    route_weights = jax.nn.softmax(route_logits, axis=-1)
    meta = route_meta(route_ids, route_weights)
    toks, hidden = project(part, residual, out_bias[None], norm_gain[None], meta)

    toks = toks.reshape(C * Z * tok_count, width + META)
    info = toks[:, width : width + 4 * top].astype(F32)
    ids, place = info[:, :top].astype(jnp.int32), info[:, top : 2 * top].astype(jnp.int32)
    weights = info[:, 2 * top : 3 * top] + info[:, 3 * top : 4 * top]
    source = jnp.arange(C * Z * tok_count, dtype=jnp.int32)[:, None] // tok_count
    slots = C * Z * capacity
    row = (ids // 8) * slots + source * capacity + place
    row = jnp.where(ids % 8 == lax.axis_index("req") % 8, row, -1)
    match = row[:, :, None] == jnp.arange(X * slots, dtype=jnp.int32)[None, None, :]
    pick = jnp.any(match, axis=1).astype(BF16)
    combine = jnp.sum(jnp.where(match, weights[:, :, None], 0.0), axis=1)
    chosen = lax.dot_general(
        pick, toks[:, :width], (((0,), (0,)), ((), ())), preferred_element_type=F32
    ).astype(BF16)
    flat_rows = spread(chosen.reshape(X, slots, width)).reshape(-1, width)

    gate_act = jnp.dot(flat_rows, gate_weight[0], preferred_element_type=F32) + gate_bias[0].astype(F32)
    up_act = jnp.dot(flat_rows, up_weight[0], preferred_element_type=F32) + up_bias[0].astype(F32)
    gate_act = jnp.minimum(gate_act, swiglu_limit)
    up_act = jnp.clip(up_act, -swiglu_limit, swiglu_limit)
    active = (gate_act * jax.nn.sigmoid(glu_alpha * gate_act) * (up_act + 1.0)).astype(BF16)
    partial_value = jnp.dot(active, down_weight[0], preferred_element_type=F32).astype(BF16)

    returned = collect(partial_value.reshape(Y, X, slots, width)).reshape(X * slots, width)
    high = combine.astype(BF16)
    low = (combine - high.astype(F32)).astype(BF16)
    mix = jnp.dot(high, returned, preferred_element_type=F32) + jnp.dot(
        low, returned, preferred_element_type=F32
    )
    expert_onehot = (
        route_ids[:, :, None] == jnp.arange(experts, dtype=jnp.int32)[None, None, :]
    ).astype(F32)
    dense_weights = jnp.einsum(
        "rk,rke->re", route_weights, expert_onehot, precision=lax.Precision.HIGHEST
    )
    base = hidden.astype(F32) + jnp.dot(
        dense_weights,
        down_bias.astype(F32),
        precision=lax.Precision.HIGHEST,
        preferred_element_type=F32,
    )
    mixed_out = finish(mix.astype(BF16).reshape(C * Z, tok_count, width), base)
    blocks = cached.reshape(-1, PAGE_LEN, cached.shape[1])
    page_pool = jnp.zeros_like(blocks).at[page_table[0]].set(blocks)
    return (mixed_out, page_pool)


def solution(mesh):
    in_specs = (
        P("req", "tp"),
        P("req", "tp"),
        P("req"),
        P("tp"),
        P("tp", None),
        P(),
        P(("req", "tp"), None),
        P(),
        P(("req", "tp"), None),
        P(("req", "tp"), None),
        P("req", None, "tp"),
        P("req", "tp"),
        P("req", None, "tp"),
        P("req", "tp"),
        P("req", "tp", None),
        P(),
        P("req", None),
    )
    out_specs = (P(("req", "tp"), None), P("req", None, "tp"))
    return jax.shard_map(body, mesh=mesh, in_specs=in_specs, out_specs=out_specs, check_vma=False)
```
